32 devices in a mesh: sample: 16 (over z, x, core), basis: 2 (over y).
Axes of the slice: x: 2, y: 2, z: 4, core: 2. Of those that a mesh axis runs over, the one named last changes fastest.
Arguments:
- points: float32 [10, 32768], P(None, 'sample'), may hold values from -1 to 1
- run_weights: float32 [32768], P('sample'), may hold values from 0.25 to 6.1
- panel_degrees: int32 [10, 128], P(None, 'basis'), may hold values from 0 to 6, as said below
- trailing_degrees: int32 [10, 512], P(None, 'basis'), may hold values from 0 to 6, as said below
Outputs:
- r_factor: float32 [128, 128], replicated
- coupling: float32 [128, 512], P(None, 'basis')
- updated: float32 [32768, 512], P('sample', 'basis')
The draws below stay inside these ranges and needn't reach their ends.
Inputs may be any that keep to these rules, and one draw needn't show every extreme that they name: `panel_degrees`: every column is a multi-index of total degree at most 6; all 640 columns are distinct. `trailing_degrees`: as for panel_degrees; no trailing column repeats a panel column.
All inputs are finite; a program needn't handle non-finite values.
Results may differ from the reference program's by a relative error of at most 0.0003.
Values sent between devices are 32-bit elements; how exact they have to be, the bound alone decides.
No kernel may reach another device: no remote copies, remote signals or barrier semaphores. Data moves between devices by JAX's collectives and lax.ppermute only.
A program may use at most 64 MiB of HBM per device.

```python
import math
import jax
import jax.numpy as jnp
import numpy as np
from jax import lax

DIMS = 10
DEG = 6
PANEL = 128
TRAIL_DEV = 256
RUNS = 32768
TRAIL = 512
N_BASIS = 2


def multi_indices(dims, top):
    if dims == 1:
        return [[degree] for degree in range(top + 1)]
    result = []
    for degree in range(top + 1):
        for tail in multi_indices(dims - 1, top - degree):
            result.append([degree] + tail)
    return result


def chosen_columns(key):
    listed = multi_indices(DIMS, DEG)
    table = jnp.asarray(np.array(listed, dtype=np.int32))
    count = len(listed)
    first_pure = [DEG] + [0] * (DIMS - 1)
    second_pure = [0, DEG] + [0] * (DIMS - 2)
    first_row = listed.index(first_pure)
    second_row = listed.index(second_pure)
    marked = np.zeros(count, dtype=np.int32)
    marked[first_row] = 1
    marked[second_row] = 1
    marked = jnp.asarray(marked)
    order = jax.random.permutation(jax.random.fold_in(key, 7), count).astype(jnp.int32)
    keys = marked[order] * count + jnp.arange(count, dtype=jnp.int32)
    others = order[jnp.argsort(keys, stable=True)][:count - 2]
    first_index = jnp.array([first_row], dtype=jnp.int32)
    second_index = jnp.array([second_row], dtype=jnp.int32)
    final_order = jnp.concatenate([first_index, others[:PANEL - 1], second_index, others[PANEL - 1:]])
    return table[final_order]


def draw_panel_degrees(key, part):
    return chosen_columns(key)[:PANEL].T


def draw_trailing_degrees(key, part):
    return chosen_columns(key)[PANEL:PANEL + TRAIL].T


def draw_points(key, part):
    return jnp.tanh(jax.random.normal(key, (DIMS, RUNS), jnp.float32))


def draw_run_weights(key, part):
    position = jnp.arange(RUNS, dtype=jnp.float32) / RUNS
    rising = 1.0 + 2.0 * position
    base = jnp.exp(jax.random.uniform(key, (RUNS,), jnp.float32, -0.7, 0.7))
    return base * rising


def setup_inputs(seed: int = 0) -> dict:
    key_list = jax.random.split(jax.random.key(seed), 5)
    points = draw_points(jax.random.fold_in(key_list[4], 71), 0)
    run_weights = draw_run_weights(jax.random.fold_in(key_list[4], 71), 0)
    panel_degrees = draw_panel_degrees(jax.random.fold_in(key_list[4], 71), 0)
    trailing_degrees = draw_trailing_degrees(jax.random.fold_in(key_list[4], 71), 0)
    return dict(points=points, run_weights=run_weights, panel_degrees=panel_degrees, trailing_degrees=trailing_degrees)


def legendre_rows(coord):
    values = [jnp.ones_like(coord), coord]
    for degree in range(1, DEG):
        values.append(((2.0 * degree + 1.0) * coord * values[degree] - degree * values[degree - 1]) / (degree + 1.0))
    return jnp.stack([values[degree] * math.sqrt(2.0 * degree + 1.0) for degree in range(DEG + 1)], axis=0)

def weighted_columns(points, degrees, weights, run_total):
    levels = jnp.arange(DEG + 1, dtype=jnp.int32)
    product = jnp.broadcast_to(jnp.sqrt(weights / run_total)[:, None], (weights.shape[0], degrees.shape[1]))
    for dim_index in range(points.shape[0]):
        table = legendre_rows(points[dim_index])
        selector = (degrees[dim_index][None, :] == levels[:, None]).astype(points.dtype)
        product = product * lax.dot_general(table, selector, (((0,), (0,)), ((), ())), precision=lax.Precision.HIGHEST)
    return product

def reference(points, run_weights, panel_degrees, trailing_degrees):
    panel = weighted_columns(points, panel_degrees, run_weights, float(RUNS))
    ortho, upper = jnp.linalg.qr(panel)
    signs = jnp.where(jnp.diagonal(upper) < 0, -1.0, 1.0).astype(upper.dtype)
    upper = upper * signs[:, None]
    ortho = ortho * signs[None, :]
    blocks = trailing_degrees.reshape(DIMS, N_BASIS, TRAIL_DEV).transpose(1, 0, 2)

    def one_block(block_degrees):
        columns = weighted_columns(points, block_degrees, run_weights, float(RUNS))
        part_coupling = lax.dot_general(ortho, columns, (((0,), (0,)), ((), ())), precision=lax.Precision.HIGHEST)
        part_update = (columns - jnp.dot(ortho, part_coupling, precision=lax.Precision.HIGHEST)) * math.sqrt(RUNS)
        return (part_coupling, part_update)
    couplings, updates = lax.map(one_block, blocks)
    coupling = couplings.transpose(1, 0, 2).reshape(PANEL, TRAIL)
    updated = updates.transpose(1, 0, 2).reshape(RUNS, TRAIL)
    return (upper, coupling, updated)
```

```python
import functools
import math

import jax
import jax.numpy as jnp
from jax import lax
from jax.experimental import pallas as pl
from jax.experimental.pallas import tpu as pltpu
from jax.sharding import PartitionSpec as P

DEG = 6
LANES = 128
F32 = jnp.float32
BF16 = jnp.bfloat16
HIGHEST = lax.Precision.HIGHEST


def rank3(a, b, c):
    all3, last2 = a + b + c, b + c
    return all3 * (all3 + 1) * (all3 + 2) // 6 + last2 * (last2 + 1) // 2 + c


def rank4(a, b, c, d):
    all4 = a + b + c + d
    return all4 * (all4 + 1) * (all4 + 2) * (all4 + 3) // 24 + rank3(b, c, d)


def codes(degrees, rows):
    d = [degrees[i] for i in range(degrees.shape[0])]
    return rows * jnp.stack([rank3(*d[0:3]), rank3(*d[3:6]), rank4(*d[6:10])])


def split2(x):
    high = x.astype(BF16)
    return high, (x - high.astype(F32)).astype(BF16)


def dot3(left, right, dims):
    (lh, ll), (rh, rl) = left, right
    go = functools.partial(lax.dot_general, dimension_numbers=(dims, ((), ())), preferred_element_type=F32)
    return go(lh, rh) + go(lh, rl) + go(ll, rh)


def levels(p):
    one = jnp.ones_like(p)
    v = [one, p]
    for k in range(1, DEG):
        v.append(((2.0 * k + 1.0) * p * v[k] - float(k) * v[k - 1]) * (1.0 / (k + 1.0)))
    return [one] + [v[k] * math.sqrt(2.0 * k + 1.0) for k in range(1, DEG + 1)]


def times(x, factor, degree):
    return x * factor[degree] if degree else x


def basis_gram(run_total, cp, ct, pts, wts, gram, basis, tab_a, tab_b, tab_c, coord, sel):
    rows = wts.shape[0]
    for d in range(pts.shape[0]):
        for i in range(rows):
            coord[pl.ds(d * rows + i, 1), :] = pts[pl.ds(d, 1), pl.ds(i * LANES, LANES)]
    scale = jnp.sqrt(wts[...] / run_total)
    lv = [levels(coord[pl.ds(d * rows, rows), :]) for d in range(pts.shape[0])]

    def put(table, rank, value):
        table[pl.ds(rank * rows, rows), :] = value

    for table, d, first in ((tab_a, 0, scale), (tab_b, 3, jnp.ones_like(scale))):
        for a in range(DEG + 1):
            xa = times(first, lv[d], a)
            for b in range(DEG + 1 - a):
                xb = times(xa, lv[d + 1], b)
                for c in range(DEG + 1 - a - b):
                    put(table, rank3(a, b, c), times(xb, lv[d + 2], c))
    for a in range(DEG + 1):
        xa = lv[6][a]
        for b in range(DEG + 1 - a):
            xb = times(xa, lv[7], b)
            for c in range(DEG + 1 - a - b):
                xc = times(xb, lv[8], c)
                for d in range(DEG + 1 - a - b - c):
                    put(tab_c, rank4(a, b, c, d), times(xc, lv[9], d))
    width, others = cp.shape[1], ct.shape[1]

    def select(code, base, count):
        unroll = 8

        def body(t, carry):
            for u in range(unroll):
                j = t * unroll + u
                a, b, c = (pl.multiple_of(code[g, j], rows) for g in range(3))
                value = tab_a[pl.ds(a, rows), :] * tab_b[pl.ds(b, rows), :] * tab_c[pl.ds(c, rows), :]
                sel[pl.ds(pl.multiple_of((base + j) * rows, rows), rows), :] = value
            return carry

        lax.fori_loop(0, count // unroll, body, 0)

    select(cp, 0, width)
    select(ct, width, others)
    total = width + others
    acc = jnp.zeros((width, total), F32)
    for i in range(rows // 2):
        x = jnp.concatenate([sel[pl.ds(2 * i + h, total, stride=rows), :] for h in range(2)], axis=1)
        basis[:, pl.ds(2 * i * LANES, 2 * LANES)] = x
        high, low = split2(x)
        acc = acc + dot3((high[:width], low[:width]), (high, low), ((1,), (1,)))
    gram[...] = acc


def factor(scale, total_ref, r_out, coupling_out, mix_out, work):
    n = total_ref.shape[0]
    block = 8
    lane = lax.broadcasted_iota(jnp.int32, (n, n), 1)
    row = lax.broadcasted_iota(jnp.int32, (n, n), 0)
    work[:, :n] = total_ref[:, :n]
    work[:, n:] = (lane == row).astype(F32)
    sub = lax.broadcasted_iota(jnp.int32, (block, n), 0)
    for k in range(n // block):
        lo = k * block
        ar = work[lo : lo + block, :]
        e = {}
        for c in range(block):
            col = jnp.broadcast_to(ar[:, lo + c : lo + c + 1], (block, n))
            for r in range(c, block):
                e[r, c] = jnp.broadcast_to(col[r : r + 1, :], (block, n))
        z, inv = {}, []
        for r in range(block):
            inv.append(lax.rsqrt(e[r, r]))
            recip = inv[r] * inv[r]
            m = {q: e[q, r] * recip for q in range(r + 1, block)}
            for q in range(r + 1, block):
                for c in range(r + 1, q + 1):
                    e[q, c] = e[q, c] - m[q] * e[c, r]
                for c in range(r):
                    z[q, c] = z[q, c] - m[q] * z[r, c]
                z[q, r] = -m[q]
        out = None
        for c in range(block):
            col = jnp.where(sub == c, inv[c], 0.0)
            for r in range(c + 1, block):
                col = jnp.where(sub == r, z[r, c] * inv[r], col)
            term = jnp.concatenate([col, col], axis=1) * jnp.broadcast_to(ar[c : c + 1, :], (block, 2 * n))
            out = term if out is None else out + term
        work[lo : lo + block, :] = out
        if k < n // block - 1:
            after = lo + block
            work[after:, :] = work[after:, :] - lax.dot_general(
                out[:, after:n], out, (((0,), (0,)), ((), ())), preferred_element_type=F32, precision=HIGHEST
            )
    r_out[...] = jnp.where(lane >= row, work[:, :n], 0.0)
    inverse = work[:, n:]
    coupling = jnp.dot(inverse, total_ref[:, n:], preferred_element_type=F32, precision=HIGHEST)
    coupling_out[...] = coupling
    mix_out[...] = scale * lax.dot_general(
        inverse, coupling, (((0,), (0,)), ((), ())), preferred_element_type=F32, precision=HIGHEST
    )


def update(scale, basis, mix, out):
    width = mix.shape[0]
    x = basis[...]
    out[...] = x[width:].T * scale - dot3(split2(x[:width]), split2(mix[...]), ((0,), (0,)))


def butterfly(x, axis, steps):
    size = lax.axis_size(axis)
    for step in steps:
        x = x + lax.ppermute(x, axis, [(i, i ^ step) for i in range(size)])
    return x


def powers(size):
    return [1 << b for b in range(size.bit_length() - 1)]


def all_sum(x, axis):
    size = lax.axis_size(axis)
    if size & (size - 1):
        return lax.psum(x, axis)
    if size == 1:
        return x
    half = x.shape[0] // 2
    odd = lax.axis_index(axis) % 2
    swap = [(i, i ^ 1) for i in range(size)]
    mine = lax.dynamic_slice_in_dim(x, odd * half, half, 0)
    mine = mine + lax.ppermute(lax.dynamic_slice_in_dim(x, (1 - odd) * half, half, 0), axis, swap)
    mine = butterfly(mine, axis, powers(size)[1:])
    other = lax.ppermute(mine, axis, swap)
    return jnp.where(odd == 0, jnp.concatenate([mine, other]), jnp.concatenate([other, mine]))


def gather_columns(x, axis):
    size = lax.axis_size(axis)
    if size & (size - 1):
        return lax.all_gather(x, axis, axis=1, tiled=True)
    full = jnp.zeros((x.shape[0], x.shape[1] * size), x.dtype)
    full = lax.dynamic_update_slice_in_dim(full, x, lax.axis_index(axis) * x.shape[1], 1)
    return butterfly(full, axis, powers(size))


def shards(points, run_weights, panel_degrees, trailing_degrees):
    runs = points.shape[1]
    rows = runs // LANES
    run_total = runs * lax.axis_size("sample")
    scale = math.sqrt(run_total)
    panel_codes = gather_columns(codes(panel_degrees, rows), "basis")
    trailing_codes = codes(trailing_degrees, rows)
    width, others = panel_codes.shape[1], trailing_codes.shape[1]
    total = width + others
    smem = pl.BlockSpec(memory_space=pltpu.SMEM)
    vmem = pl.BlockSpec(memory_space=pltpu.VMEM)
    gram, basis = pl.pallas_call(
        functools.partial(basis_gram, float(run_total)),
        out_shape=[jax.ShapeDtypeStruct((width, total), F32), jax.ShapeDtypeStruct((total, runs), F32)],
        in_specs=[smem, smem, vmem, vmem],
        out_specs=[vmem, vmem],
        scratch_shapes=[
            pltpu.VMEM((84 * rows, LANES), F32),
            pltpu.VMEM((84 * rows, LANES), F32),
            pltpu.VMEM((210 * rows, LANES), F32),
            pltpu.VMEM((points.shape[0] * rows, LANES), F32),
            pltpu.VMEM((total * rows, LANES), F32),
        ],
        compiler_params=pltpu.CompilerParams(vmem_limit_bytes=20 << 20),
        name="basis_gram",
    )(panel_codes, trailing_codes, points, run_weights.reshape(rows, LANES))
    sums = all_sum(gram, "sample")
    r_factor, coupling, mix = pl.pallas_call(
        functools.partial(factor, scale),
        out_shape=[
            jax.ShapeDtypeStruct((width, width), F32),
            jax.ShapeDtypeStruct((width, others), F32),
            jax.ShapeDtypeStruct((width, others), F32),
        ],
        in_specs=[vmem],
        out_specs=[vmem, vmem, vmem],
        scratch_shapes=[pltpu.VMEM((width, 2 * width), F32)],
        compiler_params=pltpu.CompilerParams(vmem_limit_bytes=20 << 20),
        name="factor",
    )(sums)
    tile = 2 * LANES
    updated = pl.pallas_call(
        functools.partial(update, scale),
        out_shape=jax.ShapeDtypeStruct((runs, others), F32),
        grid=(runs // tile,),
        in_specs=[pl.BlockSpec((total, tile), lambda i: (0, i)), pl.BlockSpec((width, others), lambda i: (0, 0))],
        out_specs=pl.BlockSpec((tile, others), lambda i: (i, 0)),
        compiler_params=pltpu.CompilerParams(vmem_limit_bytes=20 << 20),
        name="update",
    )(basis, mix)
    return (r_factor, coupling, updated)


def solution(mesh):
    in_specs = (P(None, "sample"), P("sample"), P(None, "basis"), P(None, "basis"))
    out_specs = (P(), P(None, "basis"), P("sample", "basis"))
    return jax.shard_map(shards, mesh=mesh, in_specs=in_specs, out_specs=out_specs, check_vma=False)
```

```python
import functools
import math

import jax
import jax.numpy as jnp
from jax import lax
from jax.experimental import pallas as pl
from jax.experimental.pallas import tpu as pltpu
from jax.sharding import PartitionSpec as P

DEG = 6
LANES = 128
BLOCK = 8
F32 = jnp.float32
BF16 = jnp.bfloat16
VMEM_LIMIT = 16 << 20


def rank3(a, b, c):
    all3, last2 = a + b + c, b + c
    return (all3 * (all3 + 1) * (all3 + 2) * 10923 >> 16) + (last2 * (last2 + 1) >> 1) + c


def rank4(a, b, c, d):
    all4 = a + b + c + d
    return (all4 * (all4 + 1) * (all4 + 2) * (all4 + 3) * 2731 >> 16) + rank3(b, c, d)


COUNT3 = rank3(0, 0, DEG) + 1
COUNT4 = rank4(0, 0, 0, DEG) + 1


def codes(degrees, rows):
    d = [degrees[i : i + 1, :] for i in range(degrees.shape[0])]
    return [rows * rank3(*d[0:3]), rows * rank3(*d[3:6]), rows * rank4(*d[6:10])]


def split2(x):
    high = x.astype(BF16)
    return high, (x - high.astype(F32)).astype(BF16)


def product(left, right, dims):
    return lax.dot_general(left, right, (dims, ((), ())), preferred_element_type=F32)


def dot3(left, right, dims):
    (lh, ll), (rh, rl) = split2(left), split2(right)
    return product(lh, rh, dims) + product(lh, rl, dims) + product(ll, rh, dims)


def levels(p):
    one = jnp.ones_like(p)
    v = [one, p]
    for k in range(1, DEG):
        v.append(((2.0 * k + 1.0) * p * v[k] - float(k) * v[k - 1]) * (1.0 / (k + 1.0)))
    return [one] + [v[k] * math.sqrt(2.0 * k + 1.0) for k in range(1, DEG + 1)]


def times(x, factor, degree):
    return x * factor[degree] if degree else x


def select(tabs, code, count, out, rows):
    for j in range(count):
        starts = [pl.multiple_of(c(j), rows) for c in code]
        a, b, c = (tab[pl.ds(s, rows), :] for tab, s in zip(tabs, starts))
        out[j * rows : (j + 1) * rows, :] = a * b * c


def tables(run_total, own_hbm, deg_hbm, pts_hbm, wts_hbm, tab_a, tab_b, tab_c, sel, own, deg, pts, wts, coord, code, code_smem, sem):
    pairs = ((deg_hbm, deg), (pts_hbm, pts), (wts_hbm, wts), (own_hbm, own))
    copies = [pltpu.make_async_copy(src, dst, sem.at[i]) for i, (src, dst) in enumerate(pairs)]
    for copy in copies:
        copy.start()
    count, rows = deg.shape[1], wts.shape[0]
    copies[0].wait()
    for g, value in enumerate(codes(deg[...], rows)):
        code[g : g + 1, :] = value
    to_scalars = pltpu.make_async_copy(code, code_smem, sem.at[len(pairs)])
    to_scalars.start()
    for copy in copies[1:]:
        copy.wait()
    for d in range(pts.shape[0]):
        for i in range(rows):
            coord[pl.ds(d * rows + i, 1), :] = pts[pl.ds(d, 1), pl.ds(i * LANES, LANES)]
    scale = jnp.sqrt(wts[...] / run_total)
    lv = [levels(coord[pl.ds(d * rows, rows), :]) for d in range(pts.shape[0])]

    def put(table, rank, value):
        table[pl.ds(rank * rows, rows), :] = value

    for table, d, first in ((tab_a, 0, scale), (tab_b, 3, jnp.ones_like(scale))):
        for a in range(DEG + 1):
            xa = times(first, lv[d], a)
            for b in range(DEG + 1 - a):
                xb = times(xa, lv[d + 1], b)
                for c in range(DEG + 1 - a - b):
                    put(table, rank3(a, b, c), times(xb, lv[d + 2], c))
    for a in range(DEG + 1):
        xa = lv[6][a]
        for b in range(DEG + 1 - a):
            xb = times(xa, lv[7], b)
            for c in range(DEG + 1 - a - b):
                xc = times(xb, lv[8], c)
                for d in range(DEG + 1 - a - b - c):
                    put(tab_c, rank4(a, b, c, d), times(xc, lv[9], d))
    to_scalars.wait()
    select((tab_a, tab_b, tab_c), [lambda j, g=g: code_smem[g, j] for g in range(3)], count, sel, rows)


def inner(rows, ca, cb, cc, tab_a, tab_b, tab_c, trail, gram, panel):
    width, others = ca.shape[0], trail.shape[0] // rows
    select((tab_a, tab_b, tab_c), [lambda j, c=c: c[j] for c in (ca, cb, cc)], width, panel, rows)
    acc = jnp.zeros((width, width + others), F32)
    for i in range(rows // 2):
        p, t = (
            jnp.concatenate([ref[pl.ds(2 * i + h, n, stride=rows), :] for h in range(2)], axis=1)
            for ref, n in ((panel, width), (trail, others))
        )
        ph, plo = split2(p)
        th, tlo = split2(t)
        high = jnp.concatenate([ph, th], axis=0)
        low = jnp.concatenate([plo, tlo], axis=0)
        dims = ((1,), (1,))
        acc = acc + product(ph, high, dims) + product(ph, low, dims) + product(plo, high, dims)
    gram[...] = acc


def by_sample(rows, scale, panel, trail, panel_halves, trail_rows):
    width, others = panel.shape[0] // rows, trail.shape[0] // rows
    for i in range(rows):
        here = pl.ds(i * LANES, LANES)
        high, low = split2(panel[pl.ds(i, width, stride=rows), :].T)
        panel_halves[here, :width] = high
        panel_halves[here, width:] = low
        trail_rows[here, :] = trail[pl.ds(i, others, stride=rows), :].T * scale


def tree(terms):
    while len(terms) > 1:
        odd = terms[-1:] if len(terms) % 2 else []
        terms = [a + b for a, b in zip(terms[::2], terms[1::2])] + odd
    return terms[0]


def small_factor(col):
    size, shape = len(col), col[0].shape
    e = {(r, c): jnp.broadcast_to(col[c][r : r + 1, :], shape) for c in range(size) for r in range(c, size)}
    x, z = {}, {}
    for r in range(size):
        inv = lax.rsqrt(e[r, r])
        for c in range(r):
            x[r, c] = z[r, c] * inv
        x[r, r] = inv
        l = {q: e[q, r] * inv for q in range(r + 1, size)}
        for q in range(r + 1, size):
            for c in range(r + 1, q + 1):
                e[q, c] = e[q, c] - l[q] * l[c]
            for c in range(r + 1):
                term = l[q] * x[r, c]
                z[q, c] = z[q, c] - term if (q, c) in z else -term
    return x


def factor_rows(a):
    b, blocks, n = BLOCK, len(a), a[0].shape[1]
    sub = lax.broadcasted_iota(jnp.int32, (b, n), 0)
    lane = lax.broadcasted_iota(jnp.int32, (b, n), 1)

    def over_lanes(v, j):
        return jnp.broadcast_to(v[:, j : j + 1], (b, n))

    def over_rows(v, r):
        return jnp.broadcast_to(v[r : r + 1, :], (b, n))

    zero = jnp.zeros((b, n), F32)
    upper, inverse = [], []
    col = [over_lanes(a[0], c) + 0.0 for c in range(b)]
    for k in range(blocks):
        lo, last = k * b, k + 1 == blocks
        f = {i: [over_lanes(a[i], lo + m) for m in range(b)] for i in range(k + 1, blocks)}
        x_col = None if last else [over_lanes(a[k + 1], lo + b + c) for c in range(b)]
        x = small_factor(col)
        if not last:
            v = [tree([f[k + 1][m] * x[c, m] for m in range(c + 1)]) for c in range(b)]
            col = [x_col[c] - tree([v[m] * over_rows(v[m], c) for m in range(b)]) for c in range(b)]
        down, across = [], []
        for c in range(b):
            p, q = zero, zero
            for r in range(c, b):
                p = jnp.where(sub == r, x[r, c], p)
            for m in range(c + 1):
                q = jnp.where(sub == m, x[c, m], q)
            down.append(p)
            across.append(q)
        t = tree([down[c] * over_rows(a[k], c) for c in range(b)])
        upper.append(jnp.where(lane >= lo + sub, t, 0.0))
        full = t
        for c in range(b):
            full = jnp.where(lane == lo + c, down[c], full)
        inverse.append(jnp.where(lane < lo + b, full, 0.0))
        if not last:
            y = tree([across[c] * over_rows(full, c) for c in range(b)])
            y_rows = [over_rows(y, m) for m in range(b)]
            inside = (lane >= lo) & (lane < lo + b)
            for i in range(k + 1, blocks):
                a[i] = jnp.where(inside, 0.0, a[i]) - tree([f[i][m] * y_rows[m] for m in range(b)])
    return upper, inverse


def finish(scale, total, panel_halves, trail_rows, r_out, coupling_out, updated_out, r_buf, c_buf, w_buf, u_buf, sem):
    n = total.shape[0]
    upper, inverse = factor_rows([total[i : i + BLOCK, :n] for i in range(0, n, BLOCK)])
    for i in range(n // BLOCK):
        r_buf[i * BLOCK : (i + 1) * BLOCK, :] = upper[i]
        w_buf[i * BLOCK : (i + 1) * BLOCK, :] = inverse[i]
    copies = [pltpu.make_async_copy(r_buf, r_out, sem.at[0])]
    copies[0].start()
    w = w_buf[...]
    coupling = dot3(w, total[:, n:], ((1,), (0,)))
    c_buf[...] = coupling
    copies.append(pltpu.make_async_copy(c_buf, coupling_out, sem.at[1]))
    copies[1].start()
    high, low = split2(scale * dot3(w, coupling, ((0,), (0,))))
    twice = jnp.concatenate([high, high], axis=0)
    runs = u_buf.shape[0]
    tile = 2 * LANES
    for i in range(runs // tile):
        here = pl.ds(i * tile, tile)
        dims = ((1,), (0,))
        u_buf[here, :] = trail_rows[here, :] - (
            product(panel_halves[here, :], twice, dims) + product(panel_halves[here, :n], low, dims)
        )
        copies.append(pltpu.make_async_copy(u_buf.at[here], updated_out.at[here], sem.at[2 + i]))
        copies[-1].start()
    for copy in copies:
        copy.wait()


def powers(size):
    return [1 << b for b in range(size.bit_length() - 1)]


def swapped(x, axis, step):
    return lax.ppermute(x, axis, [(i, i ^ step) for i in range(lax.axis_size(axis))])


def in_order(mine, other, first, dim):
    return jnp.where(first, jnp.concatenate([mine, other], dim), jnp.concatenate([other, mine], dim))


def all_sum(x, axis):
    size = lax.axis_size(axis)
    if size & (size - 1):
        return lax.psum(x, axis)
    if size == 1:
        return x
    half = x.shape[0] // 2
    odd = lax.axis_index(axis) % 2
    mine = lax.dynamic_slice_in_dim(x, odd * half, half, 0)
    mine = mine + swapped(lax.dynamic_slice_in_dim(x, (1 - odd) * half, half, 0), axis, 1)
    for step in powers(size)[1:]:
        mine = mine + swapped(mine, axis, step)
    return in_order(mine, swapped(mine, axis, 1), odd == 0, 0)


def gather_columns(x, near, axis):
    size = lax.axis_size(axis)
    if size & (size - 1):
        return lax.all_gather(x, axis, axis=1, tiled=True)
    for step in powers(size):
        other = swapped(x, axis, step)
        x = in_order(near if step == 1 else x, other, lax.axis_index(axis) & step == 0, 1)
    return x


def call(kernel, name, outs, in_specs, out_specs, scratch, args, flops, moved):
    return pl.pallas_call(
        kernel,
        out_shape=[jax.ShapeDtypeStruct(*o) for o in outs],
        in_specs=in_specs,
        out_specs=out_specs,
        scratch_shapes=scratch,
        compiler_params=pltpu.CompilerParams(vmem_limit_bytes=VMEM_LIMIT),
        cost_estimate=pl.CostEstimate(flops=flops, bytes_accessed=moved, transcendentals=0),
        name=name,
    )(*args)


def shards(points, run_weights, panel_degrees, trailing_degrees):
    dims, runs = points.shape
    rows = runs // LANES
    run_total = runs * lax.axis_size("sample")
    scale = math.sqrt(run_total)
    smem = pl.BlockSpec(memory_space=pltpu.SMEM)
    vmem = pl.BlockSpec(memory_space=pltpu.VMEM)
    far = pl.BlockSpec(memory_space=pltpu.HBM)
    own_width, others = panel_degrees.shape[1], trailing_degrees.shape[1]
    width = own_width * lax.axis_size("basis")
    total = width + others
    *tabs, trail, own_degrees = call(
        functools.partial(tables, float(run_total)),
        "tables",
        [((c * rows, LANES), F32) for c in (COUNT3, COUNT3, COUNT4, others)] + [((dims, own_width), jnp.int32)],
        [far] * 4,
        [vmem] * 5,
        [
            pltpu.VMEM((dims, others), jnp.int32),
            pltpu.VMEM((dims, runs), F32),
            pltpu.VMEM((rows, LANES), F32),
            pltpu.VMEM((dims * rows, LANES), F32),
            pltpu.VMEM((BLOCK, others), jnp.int32),
            pltpu.SMEM((BLOCK, others), jnp.int32),
            pltpu.SemaphoreType.DMA((5,)),
        ],
        [
            pltpu.with_memory_space_constraint(x, pltpu.HBM)
            for x in (panel_degrees, trailing_degrees, points, run_weights.reshape(rows, LANES))
        ],
        runs * 1000,
        runs * 2000,
    )
    all_degrees = gather_columns(panel_degrees, own_degrees, "basis")
    gram, panel = call(
        functools.partial(inner, rows),
        "inner",
        [((width, total), F32), ((width * rows, LANES), F32)],
        [smem] * 3 + [vmem] * 4,
        [vmem] * 2,
        [],
        (*(c[0] for c in codes(all_degrees, rows)), *tabs, trail),
        6 * width * total * runs,
        4 * runs * total,
    )
    panel_halves, trail_rows = call(
        functools.partial(by_sample, rows, scale),
        "by_sample",
        [((runs, 2 * width), BF16), ((runs, others), F32)],
        [vmem] * 2,
        [vmem] * 2,
        [],
        (panel, trail),
        runs * total,
        8 * runs * total,
    )
    sums = all_sum(gram, "sample")
    r_factor, coupling, updated = call(
        functools.partial(finish, scale),
        "finish",
        [((width, width), F32), ((width, others), F32), ((runs, others), F32)],
        [vmem] * 3,
        [far] * 3,
        [
            pltpu.VMEM((width, width), F32),
            pltpu.VMEM((width, others), F32),
            pltpu.VMEM((width, width), F32),
            pltpu.VMEM((runs, others), F32),
            pltpu.SemaphoreType.DMA((2 + runs // (2 * LANES),)),
        ],
        (sums, panel_halves, trail_rows),
        6 * width * others * runs,
        8 * runs * total,
    )
    return (r_factor, coupling, updated)


def solution(mesh):
    in_specs = (P(None, "sample"), P("sample"), P(None, "basis"), P(None, "basis"))
    out_specs = (P(), P(None, "basis"), P("sample", "basis"))
    return jax.shard_map(shards, mesh=mesh, in_specs=in_specs, out_specs=out_specs, check_vma=False)
```
